32 devices in a mesh: rep: 2 (over y), shard: 16 (over z, x, core).
Axes of the slice: x: 2, y: 2, z: 4, core: 2. Of those that a mesh axis runs over, the one named last changes fastest.
Arguments:
- layer_input: bfloat16 [4096, 1024], P(('rep', 'shard')), may hold values from -6 to 6
- out_cotangent: bfloat16 [4096, 1024], P(('rep', 'shard')), may hold values from -6 to 6
- segment_ids: int32 [4096], P(('rep', 'shard')), may hold values from -1 to 4, as said below
- weights: float32 [1024, 12288], P('shard')
- weight_m: float32 [1024, 12288], P('shard'), may hold values from -18 to 18
- weight_v: float32 [1024, 12288], P('shard'), may hold values from 0.5 to 5
- vectors: float32 [1024, 12], P('shard')
- vector_m: float32 [1024, 12], P('shard'), may hold values from -18 to 18
- vector_v: float32 [1024, 12], P('shard'), may hold values from 0.5 to 5
Outputs:
- layer_output: bfloat16 [4096, 1024], P(('rep', 'shard'))
- input_grad: float32 [4096, 1024], P(('rep', 'shard'))
- weight_grad: float32 [1024, 12288], P('shard')
- new_weights: float32 [1024, 12288], P('shard')
- new_weight_m: float32 [1024, 12288], P('shard')
- new_weight_v: float32 [1024, 12288], P('shard')
- vector_grad: float32 [1024, 12], P('shard')
- new_vectors: float32 [1024, 12], P('shard')
- new_vector_m: float32 [1024, 12], P('shard')
- new_vector_v: float32 [1024, 12], P('shard')
The draws below stay inside these ranges and needn't reach their ends.
Inputs may be any that keep to these rules, and one draw needn't show every extreme that they name: `segment_ids`: within each device's 128 slots the live slots come first, numbered by sequence 0, 1, ... in order, and padding slots follow with -1. The slots of each device are cut into sequences at 4 distinct places, so a device without padding holds sequence numbers 0 to 4; some device has no padding.
All inputs are finite; a program needn't handle non-finite values.
Results may differ from the reference program's by a relative error of at most 0.014.
The reference program's roundings to bfloat16 on the way count: a program that leaves them out, or rounds other values in their place, can miss the bound.
Values may be sent and summed in bfloat16 or wider, within the bound.
No kernel may reach another device: no remote copies, remote signals or barrier semaphores. Data moves between devices by JAX's collectives and lax.ppermute only.
A program may use at most 192 MiB of HBM per device.

```python
import math
import jax
import jax.numpy as jnp
from jax import lax

D = 1024
HEAD_DIM = 64
FF = 4096
ROWS = 128
ADAM_STEP = 3
WCOLS = 12288
VCOLS = 12
TOKENS = 4096


def draw_segment_ids(key, part):
    blocks = TOKENS // ROWS
    cut_count = max(1, ROWS // 32)
    key_fill = jax.random.fold_in(key, 101)
    key_cut = jax.random.fold_in(key, 102)
    key_full = jax.random.fold_in(key, 103)
    live_rows = jax.random.randint(key_fill, (blocks,), ROWS // 4, ROWS + 1)
    dealt_order = jax.random.permutation(key_full, blocks)
    live_rows = jnp.where(dealt_order == 0, ROWS, live_rows)
    cut_keys = jax.random.split(key_cut, blocks)
    orders = jax.vmap(lambda one_key: jax.random.permutation(one_key, ROWS - 1))(cut_keys)
    cut_spots = orders[:, :cut_count] + 1
    positions = jnp.arange(ROWS, dtype=jnp.int32)
    cut_marks = jnp.any(cut_spots[:, :, None] == positions[None, None, :], axis=1)
    seg_ids = jnp.cumsum(cut_marks.astype(jnp.int32), axis=1)
    seg_ids = jnp.where(positions[None, :] < live_rows[:, None], seg_ids, -1)
    return seg_ids.reshape(-1).astype(jnp.int32)


def draw_layer_input(key, part):
    own_key = jax.random.fold_in(key, 201)
    mixed = jax.random.normal(own_key, (TOKENS, D), jnp.float32)
    return jnp.clip(mixed, -6.0, 6.0).astype(jnp.bfloat16)


def draw_weights(key, part):
    own_key = jax.random.fold_in(key, 301)
    col_count = 4 * D + 2 * FF
    column = jnp.arange(col_count)
    col_scale = jnp.where(column < 3 * D, D ** (-0.5), jnp.where(column < 4 * D, 4.0 * D ** (-0.5), jnp.where(column < 4 * D + FF, D ** (-0.5), FF ** (-0.5))))
    base_draw = jax.random.normal(own_key, (D, col_count), jnp.float32)
    return (base_draw * col_scale[None, :].astype(jnp.float32)).astype(jnp.float32)


def draw_vectors(key, part):
    own_key = jax.random.fold_in(key, 401)
    col_count = 8 + FF // D
    column = jnp.arange(col_count)
    is_gain = (column == 3) | (column == col_count - 2)
    base_draw = jnp.clip(jax.random.normal(own_key, (D, col_count), jnp.float32), -3.0, 3.0)
    return jnp.where(is_gain[None, :], 1.0 + 0.2 * base_draw, 0.5 * base_draw).astype(jnp.float32)


def block_levels(key, shape, pieces, least, largest):
    def one(position, parts):
        steps = jax.random.uniform(jax.random.fold_in(jax.random.fold_in(key, 6), position), (parts,), jnp.float32, least / len(pieces), largest / len(pieces))
        return jnp.repeat(jnp.exp(steps), shape[position] // parts).reshape((-1,) + (1,) * (len(shape) - position - 1))

    level = one(*pieces[0])
    for cut in pieces[1:]:
        level = level * one(*cut)
    return level


def noise(key, shape, width, bound, pieces=(), kind=jnp.bfloat16):
    level = block_levels(key, shape, pieces, -0.22, 0.18) if pieces else 1.0
    result = jax.random.normal(key, shape, jnp.float32) * width * level
    return jnp.minimum(jnp.maximum(result, -bound), bound).astype(kind)


def setup_inputs(seed: int = 0) -> dict:
    streams_of = jax.random.split(jax.random.key(seed), 10)
    return {
        "layer_input": draw_layer_input(jax.random.fold_in(streams_of[9], 71), 0),
        "out_cotangent": noise(streams_of[1], (TOKENS, D), 1.0, 6.0, ((0, 32),)),
        "segment_ids": draw_segment_ids(jax.random.fold_in(streams_of[9], 71), 0),
        "weights": draw_weights(jax.random.fold_in(streams_of[9], 71), 0),
        "weight_m": noise(streams_of[4], (D, WCOLS), 3.0, 18.0, ((0, 16),), jnp.float32),
        "weight_v": jnp.clip(jnp.exp(math.log(5.0) - 2.3025851 * jax.random.uniform(streams_of[5], (D, WCOLS), jnp.float32) ** block_levels(streams_of[5], (D, WCOLS), ((0, 16),), -0.2, 0.2)), 0.5, 5.0),
        "vectors": draw_vectors(jax.random.fold_in(streams_of[9], 71), 0),
        "vector_m": noise(streams_of[7], (D, VCOLS), 3.0, 18.0, ((0, 16),), jnp.float32),
        "vector_v": jnp.clip(jnp.exp(math.log(5.0) - 2.3025851 * jax.random.uniform(streams_of[8], (D, VCOLS), jnp.float32) ** block_levels(streams_of[8], (D, VCOLS), ((0, 16),), -0.2, 0.2)), 0.5, 5.0),
    }


norm_eps = 1e-05
beta_one = 0.9
beta_two = 0.999
matrix_rate = 0.004
vector_rate = 0.1
weight_decay = 0.01

def product(einsum_form, first_op, second_op):
    return jnp.einsum(einsum_form, first_op.astype(jnp.float32), second_op.astype(jnp.float32))

def cross_dot(first_op, second_op):
    return lax.dot_general(first_op, second_op, (((0,), (0,)), ((), ())), preferred_element_type=jnp.float32)

def trans_dot(first_op, second_op):
    return lax.dot_general(first_op, second_op, (((1,), (1,)), ((), ())), preferred_element_type=jnp.float32)

def gelu_exact(values_in):
    return jax.nn.gelu(values_in, approximate=False)

def norm_rows(total_in, gain, shift):
    row_mean = lax.optimization_barrier(jnp.mean(total_in, axis=-1, keepdims=True))
    centered = total_in - row_mean
    inverse = lax.rsqrt(lax.optimization_barrier(jnp.mean(centered * centered, axis=-1, keepdims=True)) + norm_eps)
    unit_rows = centered * inverse
    return (unit_rows * gain + shift, unit_rows, inverse)

def norm_back(grad_unit, unit_rows, inverse):
    return inverse * (grad_unit - lax.optimization_barrier(jnp.mean(grad_unit, axis=-1, keepdims=True)) - unit_rows * lax.optimization_barrier(jnp.mean(grad_unit * unit_rows, axis=-1, keepdims=True)))

def split_vectors(small_params):
    col_count = small_params.shape[1]
    up_bias = small_params[:, 5:col_count - 3].T.reshape(-1)
    return (small_params[:, 0], small_params[:, 1], small_params[:, 2], small_params[:, 3], small_params[:, 4], up_bias, small_params[:, col_count - 3], small_params[:, col_count - 2], small_params[:, col_count - 1])

def pack_vectors(query_bias, value_bias, output_bias, first_gain, first_shift, up_bias, down_bias, second_gain, second_shift):
    model_width = query_bias.shape[0]
    head_part = jnp.stack([query_bias, value_bias, output_bias, first_gain, first_shift], axis=1)
    tail_part = jnp.stack([down_bias, second_gain, second_shift], axis=1)
    return jnp.concatenate([head_part, up_bias.reshape(-1, model_width).T, tail_part], axis=1)

def split_matrices(packed, model_width, hidden):
    return (packed[:, :3 * model_width], packed[:, 3 * model_width:4 * model_width], packed[:, 4 * model_width:4 * model_width + hidden], packed[:, 4 * model_width + hidden:])

def masked_scores(query_rows, key_rows, seg_ids):
    score_scale = query_rows.shape[-1] ** (-0.5)
    scores = product('qhe,khe->hqk', query_rows, key_rows) * score_scale
    same_seq = seg_ids[:, None] == seg_ids[None, :]
    return jnp.where(same_seq[None], scores, -1e+30)

def attend_rows(query_rows, key_rows, values, seg_ids):
    scores = masked_scores(query_rows, key_rows, seg_ids)
    row_top = lax.optimization_barrier(jnp.max(scores, axis=-1, keepdims=True))
    log_total = row_top + jnp.log(lax.optimization_barrier(jnp.sum(jnp.exp(scores - row_top), axis=-1, keepdims=True)))
    attn_probs = jnp.exp(scores - log_total).astype(jnp.bfloat16)
    context = product('hqk,khe->qhe', attn_probs, values).astype(jnp.bfloat16)
    return (context, log_total)

def attend_back(query_rows, key_rows, values, seg_ids, log_total, grad_context):
    score_scale = query_rows.shape[-1] ** (-0.5)
    scores = masked_scores(query_rows, key_rows, seg_ids)
    attn_probs = jnp.exp(scores - log_total)
    probs_low = attn_probs.astype(jnp.bfloat16)
    grad_probs = product('qhe,khe->hqk', grad_context, values)
    grad_scores = attn_probs * (grad_probs - lax.optimization_barrier(jnp.sum(attn_probs * grad_probs, axis=-1, keepdims=True)))
    grad_scores = (grad_scores * score_scale).astype(jnp.bfloat16)
    grad_query = product('hqk,khe->qhe', grad_scores, key_rows)
    grad_keys = product('hqk,qhe->khe', grad_scores, query_rows)
    grad_values = product('hqk,qhe->khe', probs_low, grad_context)
    return (grad_query, grad_keys, grad_values)

def forward_pass(rows_in, rows_seg, matrices, small_params):
    w_qkv, w_out, w_up, w_down = matrices
    groups, row_count, model_width = rows_in.shape
    head_count = model_width // HEAD_DIM
    query_bias, value_bias, output_bias, first_gain, first_shift, up_bias, down_bias, second_gain, second_shift = split_vectors(small_params)
    flat_in = rows_in.reshape(groups * row_count, model_width)
    mixed_qkv = jnp.dot(flat_in, w_qkv, preferred_element_type=jnp.float32)
    head_shape = (groups, row_count, head_count, HEAD_DIM)
    query_rows = (mixed_qkv[:, :model_width] + query_bias).astype(jnp.bfloat16).reshape(head_shape)
    key_rows = mixed_qkv[:, model_width:2 * model_width].astype(jnp.bfloat16).reshape(head_shape)
    values = (mixed_qkv[:, 2 * model_width:] + value_bias).astype(jnp.bfloat16).reshape(head_shape)
    context, log_total = jax.vmap(attend_rows)(query_rows, key_rows, values, rows_seg)
    context = context.reshape(groups * row_count, model_width)
    attended = jnp.dot(context, w_out, preferred_element_type=jnp.float32) + output_bias
    first_sum = flat_in.astype(jnp.float32) + attended
    normed, first_unit, first_inv = norm_rows(first_sum, first_gain, first_shift)
    normed_low = normed.astype(jnp.bfloat16)
    up_proj = jnp.dot(normed_low, w_up, preferred_element_type=jnp.float32) + up_bias
    active = gelu_exact(up_proj).astype(jnp.bfloat16)
    down_proj = trans_dot(active, w_down) + down_bias
    second_sum = normed + down_proj
    final_rows, second_unit, second_inv = norm_rows(second_sum, second_gain, second_shift)
    valid_rows = (rows_seg.reshape(-1) >= 0)[:, None]
    output = jnp.where(valid_rows, final_rows, 0.0).astype(jnp.bfloat16).reshape(groups, row_count, model_width)
    saved_state = (flat_in, rows_seg, query_rows, key_rows, values, log_total, context, first_unit, first_inv, normed_low, up_proj, active, second_unit, second_inv, valid_rows)
    return (output, saved_state)

def backward_pass(saved_state, rows_cot, matrices, small_params):
    w_qkv, w_out, w_up, w_down = matrices
    flat_in, rows_seg, query_rows, key_rows, values, log_total, context, first_unit, first_inv, normed_low, up_proj, active, second_unit, second_inv, valid_rows = saved_state
    groups, row_count, head_count, head_size = query_rows.shape
    model_width = head_count * head_size
    query_bias, value_bias, output_bias, first_gain, first_shift, up_bias, down_bias, second_gain, second_shift = split_vectors(small_params)
    grad_final = jnp.where(valid_rows, rows_cot.reshape(-1, model_width).astype(jnp.float32), 0.0)
    grad_second_gain = lax.optimization_barrier(jnp.sum(grad_final * second_unit, axis=0))
    grad_second_shift = lax.optimization_barrier(jnp.sum(grad_final, axis=0))
    grad_second = norm_back(grad_final * second_gain, second_unit, second_inv)
    grad_down_bias = lax.optimization_barrier(jnp.sum(grad_second, axis=0))
    grad_second_low = grad_second.astype(jnp.bfloat16)
    grad_active = jnp.dot(grad_second_low, w_down, preferred_element_type=jnp.float32)
    grad_up = jax.vjp(gelu_exact, up_proj)[1](grad_active)[0]
    grad_up_bias = lax.optimization_barrier(jnp.sum(grad_up, axis=0))
    grad_up_low = grad_up.astype(jnp.bfloat16)
    grad_normed = grad_second + trans_dot(grad_up_low, w_up)
    grad_first_gain = lax.optimization_barrier(jnp.sum(grad_normed * first_unit, axis=0))
    grad_first_shift = lax.optimization_barrier(jnp.sum(grad_normed, axis=0))
    grad_first = norm_back(grad_normed * first_gain, first_unit, first_inv)
    grad_output_bias = lax.optimization_barrier(jnp.sum(grad_first, axis=0))
    grad_first_low = grad_first.astype(jnp.bfloat16)
    grad_context = trans_dot(grad_first_low, w_out)
    grad_context = grad_context.astype(jnp.bfloat16).reshape(groups, row_count, head_count, head_size)
    grad_query, grad_keys, grad_values = jax.vmap(attend_back)(query_rows, key_rows, values, rows_seg, log_total, grad_context)
    flat_shape = (groups * row_count, model_width)
    grad_query = grad_query.reshape(flat_shape)
    grad_values = grad_values.reshape(flat_shape)
    grad_mixed = jnp.concatenate([grad_query, grad_keys.reshape(flat_shape), grad_values], axis=1).astype(jnp.bfloat16)
    grad_input = grad_first + trans_dot(grad_mixed, w_qkv)
    grad_parts = (cross_dot(flat_in, grad_mixed), cross_dot(context, grad_first_low), cross_dot(normed_low, grad_up_low), cross_dot(grad_second_low, active))
    grad_small = pack_vectors(lax.optimization_barrier(jnp.sum(grad_query, axis=0)), lax.optimization_barrier(jnp.sum(grad_values, axis=0)), grad_output_bias, grad_first_gain, grad_first_shift, grad_up_bias, grad_down_bias, grad_second_gain, grad_second_shift)
    return (grad_input, grad_parts, grad_small)

def adam_step(param_now, moment_now, second_now, grad_now, rate, decay):
    moment_new = beta_one * moment_now + (1.0 - beta_one) * grad_now
    second_new = beta_two * second_now + (1.0 - beta_two) * grad_now * grad_now
    moment_hat = moment_new / (1.0 - beta_one ** ADAM_STEP)
    second_hat = second_new / (1.0 - beta_two ** ADAM_STEP)
    param_new = param_now - rate * (moment_hat / (jnp.sqrt(second_hat) + 1e-08) + decay * param_now)
    return (param_new, moment_new, second_new)

def reference(layer_input, out_cotangent, segment_ids, weights, weight_m, weight_v, vectors, vector_m, vector_v):
    blocks = TOKENS // ROWS
    block_limit = max(1, 4096 // ROWS)
    group_size = math.gcd(blocks, 1 << block_limit.bit_length() - 1)
    matrices = split_matrices(weights.astype(jnp.bfloat16), D, FF)
    small_params = lax.optimization_barrier(vectors.astype(jnp.bfloat16)).astype(jnp.float32)
    shaped_in = layer_input.reshape(blocks // group_size, group_size, ROWS, D)
    shaped_cot = out_cotangent.reshape(blocks // group_size, group_size, ROWS, D)
    shaped_seg = segment_ids.reshape(blocks // group_size, group_size, ROWS)

    def scan_step(grad_sums, block_data):
        rows_in, rows_cot, rows_seg = block_data
        output, saved_state = forward_pass(rows_in, rows_seg, matrices, small_params)
        grad_input, grad_parts, grad_small = backward_pass(saved_state, rows_cot, matrices, small_params)
        new_sums = tuple((total + term for total, term in zip(grad_sums[0], grad_parts)))
        return ((new_sums, grad_sums[1] + grad_small), (output, grad_input))
    start_parts = tuple((jnp.zeros((D, piece.shape[1]), jnp.float32) for piece in matrices))
    start_sums = (start_parts, jnp.zeros((D, VCOLS), jnp.float32))
    (grad_parts, grad_small), (outputs, grads_in) = lax.scan(scan_step, start_sums, (shaped_in, shaped_cot, shaped_seg))
    grad_wide = jnp.concatenate(grad_parts, axis=1)
    new_w, new_wm, new_wv = adam_step(weights, weight_m, weight_v, grad_wide, matrix_rate, weight_decay)
    new_vec, new_vm, new_vv = adam_step(vectors, vector_m, vector_v, grad_small, vector_rate, 0.0)
    return (outputs.reshape(TOKENS, D), grads_in.reshape(TOKENS, D), grad_wide, new_w, new_wm, new_wv, grad_small, new_vec, new_vm, new_vv)
```

```python
import jax
import jax.numpy as jnp
from jax import lax
from jax.sharding import PartitionSpec as P

HEAD_DIM = 64
ADAM_STEP = 3

norm_eps = 1e-05
beta_one = 0.9
beta_two = 0.999
matrix_rate = 0.004
vector_rate = 0.1
weight_decay = 0.01

AXES = ("rep", "shard")

f32 = jnp.float32
bf16 = jnp.bfloat16


def dot(a, b):
    return lax.dot_general(a, b, (((1,), (0,)), ((), ())), preferred_element_type=f32)


def cross_dot(a, b):
    return lax.dot_general(a, b, (((0,), (0,)), ((), ())), preferred_element_type=f32)


def trans_dot(a, b):
    return lax.dot_general(a, b, (((1,), (1,)), ((), ())), preferred_element_type=f32)


def product(form, a, b):
    return jnp.einsum(form, a, b, preferred_element_type=f32)


def gelu_exact(x):
    return jax.nn.gelu(x, approximate=False)


def norm_rows(total_in, gain, shift):
    row_mean = jnp.mean(total_in, axis=-1, keepdims=True)
    centered = total_in - row_mean
    inverse = lax.rsqrt(jnp.mean(centered * centered, axis=-1, keepdims=True) + norm_eps)
    unit_rows = centered * inverse
    return (unit_rows * gain + shift, unit_rows, inverse)


def norm_back(grad_unit, unit_rows, inverse):
    return inverse * (
        grad_unit
        - jnp.mean(grad_unit, axis=-1, keepdims=True)
        - unit_rows * jnp.mean(grad_unit * unit_rows, axis=-1, keepdims=True)
    )


def masked_scores(query_rows, key_rows, seg_ids):
    scores = product("bqhe,bkhe->bhqk", query_rows, key_rows) * HEAD_DIM ** (-0.5)
    same_seq = seg_ids[:, :, None] == seg_ids[:, None, :]
    return jnp.where(same_seq[:, None], scores, -1e30)


def attend_rows(query_rows, key_rows, values, seg_ids):
    scores = masked_scores(query_rows, key_rows, seg_ids)
    row_top = jnp.max(scores, axis=-1, keepdims=True)
    log_total = row_top + jnp.log(jnp.sum(jnp.exp(scores - row_top), axis=-1, keepdims=True))
    probs = jnp.exp(scores - log_total).astype(bf16)
    return product("bhqk,bkhe->bqhe", probs, values).astype(bf16), log_total


def attend_back(query_rows, key_rows, values, seg_ids, log_total, grad_context):
    scores = masked_scores(query_rows, key_rows, seg_ids)
    probs = jnp.exp(scores - log_total)
    probs_low = probs.astype(bf16)
    grad_probs = product("bqhe,bkhe->bhqk", grad_context, values)
    grad_scores = probs * (grad_probs - jnp.sum(probs * grad_probs, axis=-1, keepdims=True))
    grad_scores = (grad_scores * HEAD_DIM ** (-0.5)).astype(bf16)
    grad_query = product("bhqk,bkhe->bqhe", grad_scores, key_rows)
    grad_keys = product("bhqk,bqhe->bkhe", grad_scores, query_rows)
    grad_values = product("bhqk,bqhe->bkhe", probs_low, grad_context)
    return grad_query, grad_keys, grad_values


def adam_step(param_now, moment_now, second_now, grad_now, rate, decay):
    moment_new = beta_one * moment_now + (1.0 - beta_one) * grad_now
    second_new = beta_two * second_now + (1.0 - beta_two) * grad_now * grad_now
    moment_hat = moment_new / (1.0 - beta_one**ADAM_STEP)
    second_hat = second_new / (1.0 - beta_two**ADAM_STEP)
    param_new = param_now - rate * (moment_hat / (jnp.sqrt(second_hat) + 1e-08) + decay * param_now)
    return (param_new, moment_new, second_new)


class Links:
    def __init__(self, rep_count, shard_count):
        self.rep_count = rep_count
        self.shard_count = shard_count
        self.chips = shard_count // 2
        self.ring = self.chips // 2
        shard = lax.axis_index("shard")
        self.core = shard % 2
        self.chip = shard // 2
        self.ring_at = self.chip // 2
        self.pair_at = self.chip % 2

    def _pairs(self, step):
        pairs = []
        for rep in range(self.rep_count):
            for ring_at in range(self.ring):
                for pair_at in range(2):
                    for core in range(2):
                        r, z, x, c = step(rep, ring_at, pair_at, core)
                        pairs.append(
                            (
                                rep * self.shard_count + (ring_at * 2 + pair_at) * 2 + core,
                                r * self.shard_count + ((z % self.ring) * 2 + x) * 2 + c,
                            )
                        )
        return pairs

    def _send(self, value, step):
        return lax.ppermute(value, AXES, self._pairs(step))

    def swap_core(self, value):
        return self._send(value, lambda r, z, x, c: (r, z, x, 1 - c))

    def swap_pair(self, value):
        return self._send(value, lambda r, z, x, c: (r, z, 1 - x, c))

    def up(self, value):
        return self._send(value, lambda r, z, x, c: (r, z + 1, x, c))

    def down(self, value):
        return self._send(value, lambda r, z, x, c: (r, z - 1, x, c))

    def swap_rep(self, value, bit):
        return self._send(value, lambda r, z, x, c: (r ^ bit, z, x, c))

    def sum_all(self, value):
        total = self.rep_count * self.shard_count
        bit = 1
        while bit < total:
            pairs = [(i, i ^ bit) for i in range(total)]
            value = value + lax.ppermute(value, AXES, pairs)
            bit *= 2
        return value

    def to_own_order(self, value, axis, first_offset=0):
        width = value.shape[axis] // self.chips
        pieces = []
        for dist in range(self.ring):
            for flip in range(2):
                block = ((self.ring_at + dist) % self.ring) * 2 + (self.pair_at ^ flip)
                block = (block + first_offset) % self.chips
                pieces.append(lax.dynamic_slice_in_dim(value, block * width, width, axis))
        return jnp.concatenate(pieces, axis=axis)

    def to_plain_order(self, value, axis):
        width = value.shape[axis] // self.chips
        pieces = []
        for ring_at in range(self.ring):
            for pair_at in range(2):
                block = ((ring_at - self.ring_at) % self.ring) * 2 + (self.pair_at ^ pair_at)
                pieces.append(lax.dynamic_slice_in_dim(value, block * width, width, axis))
        return jnp.concatenate(pieces, axis=axis)

    def gather(self, own):
        ring = self.ring
        half = own.shape[0] // 2
        blocks = {}
        near = (own, self.swap_pair(own))
        blocks[0] = near
        ups, downs = near, near
        for dist in range(1, (ring + 1) // 2):
            ups = tuple(self.up(part) for part in ups)
            downs = tuple(self.down(part) for part in downs)
            blocks[ring - dist] = ups
            blocks[dist] = downs
        if ring % 2 == 0:
            top = self.up(ups[0][:half])
            low = self.down(downs[0][half:])
            blocks[ring // 2] = (top, low, self.swap_pair(top), self.swap_pair(low))
        return jnp.concatenate([part for dist in range(ring) for part in blocks[dist]], axis=0)

    def scatter(self, terms):
        ring = self.ring
        width = terms.shape[0] // self.chips
        half = width // 2

        def block(dist, flip):
            first = ((dist % ring) * 2 + flip) * width
            return terms[first : first + width]

        def add(a, b):
            return (a.astype(f32) + b.astype(f32)).astype(bf16)

        far_up = far_down = None
        if ring % 2 == 0:
            far = add(block(ring // 2, 0), self.swap_pair(block(ring // 2, 1)))
            far_up = self.up(far[:half])
            far_down = self.down(far[half:])
        last = (ring - 1) // 2
        ups = [block(last, 0), block(last, 1)]
        downs = [block(-last, 0), block(-last, 1)]
        if last == 0:
            here = ups
            if far_up is not None:
                here = [add(here[0], jnp.concatenate([far_up, far_down], axis=0)), here[1]]
        else:
            if far_up is not None:
                ups[0] = jnp.concatenate([add(ups[0][:half], far_up), ups[0][half:]], axis=0)
                downs[0] = jnp.concatenate(
                    [downs[0][:half], add(downs[0][half:], far_down)], axis=0
                )
            for dist in range(last, 0, -1):
                from_low = [self.up(part) for part in ups]
                from_high = [self.down(part) for part in downs]
                if dist > 1:
                    ups = [add(block(dist - 1, i), from_low[i]) for i in range(2)]
                    downs = [add(block(1 - dist, i), from_high[i]) for i in range(2)]
            here = [
                (
                    block(0, i).astype(f32)
                    + from_low[i].astype(f32)
                    + from_high[i].astype(f32)
                ).astype(bf16)
                for i in range(2)
            ]
        return add(here[0], self.swap_pair(here[1]))


def body(
    layer_input,
    out_cotangent,
    segment_ids,
    weights,
    weight_m,
    weight_v,
    vectors,
    vector_m,
    vector_v,
    rep_count,
    shard_count,
):
    links = Links(rep_count, shard_count)
    first_core = links.core == 0
    row_count, width = layer_input.shape
    own_rows, vec_cols = vectors.shape
    hidden = (weights.shape[1] - 4 * width) // 2
    hw = width // 2
    hh = hidden // 2
    heads = hw // HEAD_DIM

    def pick(low, high):
        return jnp.where(first_core, low, high)

    def both(own, other, axis):
        return pick(
            jnp.concatenate([own, other], axis=axis), jnp.concatenate([other, own], axis=axis)
        )

    def halves(value, axis=-1):
        low, high = jnp.split(value, 2, axis=axis)
        return pick(low, high), pick(high, low)

    wide = weights.astype(bf16)
    parts = {
        "qkv": wide[:, : 3 * width].reshape(own_rows, 3, width),
        "out": wide[:, 3 * width : 4 * width],
        "up": wide[:, 4 * width : 4 * width + hidden],
        "down": wide[:, 4 * width + hidden :],
    }
    small_low = vectors.astype(bf16)
    small_pad = jnp.pad(small_low, ((0, 0), (0, -vec_cols % 128)))

    def chip_block(name):
        mine, theirs = halves(parts[name])
        mine = mine.reshape(own_rows, -1)
        theirs = theirs.reshape(own_rows, -1)
        if name == "qkv":
            mine = jnp.concatenate([mine, small_pad], axis=1)
            theirs = jnp.concatenate([theirs, small_pad], axis=1)
        return both(mine, links.swap_core(theirs), 0)

    w_first = links.gather(chip_block("qkv"))
    w_qkv = w_first[:, : 3 * hw]
    small = links.to_plain_order(w_first[:, 3 * hw : 3 * hw + vec_cols].astype(f32), 0).T
    w_out = links.gather(chip_block("out"))
    w_up = links.gather(chip_block("up"))
    w_down = links.gather(chip_block("down"))

    query_bias, value_bias = halves(small[0])[0], halves(small[1])[0]
    output_bias, first_gain, first_shift = small[2], small[3], small[4]
    up_bias = halves(small[5 : vec_cols - 3].reshape(-1))[0]
    down_bias, second_gain, second_shift = (
        small[vec_cols - 3],
        small[vec_cols - 2],
        small[vec_cols - 1],
    )

    def chip_tokens(own):
        return jnp.concatenate([own, links.swap_core(own)], axis=0)

    def sum_cores(value):
        return value[:row_count] + links.swap_core(value[row_count:])

    rows_in = links.to_own_order(chip_tokens(layer_input), 1)
    seg = chip_tokens(segment_ids).reshape(2, row_count)
    mixed = dot(rows_in, w_qkv)
    head_shape = (2, row_count, heads, HEAD_DIM)
    query_rows = (mixed[:, :hw] + query_bias).astype(bf16).reshape(head_shape)
    key_rows = mixed[:, hw : 2 * hw].astype(bf16).reshape(head_shape)
    values = (mixed[:, 2 * hw :] + value_bias).astype(bf16).reshape(head_shape)
    context, log_total = attend_rows(query_rows, key_rows, values, seg)
    context = context.reshape(2 * row_count, hw)
    other = links.swap_core(context)
    other = jnp.concatenate([other[row_count:], other[:row_count]], axis=0)
    context = links.to_own_order(both(context, other, 1), 1)
    attended = dot(context, w_out)
    attended = both(attended[:row_count], links.swap_core(attended[row_count:]), 1)
    first_sum = layer_input.astype(f32) + (attended + output_bias)
    normed, first_unit, first_inv = norm_rows(first_sum, first_gain, first_shift)
    normed_low = links.to_own_order(chip_tokens(normed.astype(bf16)), 1)
    up_proj = dot(normed_low, w_up) + up_bias
    active = gelu_exact(up_proj).astype(bf16)
    down_proj = links.to_plain_order(sum_cores(trans_dot(active, w_down)), 1)
    second_sum = normed + (down_proj + down_bias)
    final_rows, second_unit, second_inv = norm_rows(second_sum, second_gain, second_shift)
    valid_rows = (segment_ids >= 0)[:, None]
    output = jnp.where(valid_rows, final_rows, 0.0).astype(bf16)

    grad_final = jnp.where(valid_rows, out_cotangent.astype(f32), 0.0)
    grad_second_gain = jnp.sum(grad_final * second_unit, axis=0)
    grad_second_shift = jnp.sum(grad_final, axis=0)
    grad_second = norm_back(grad_final * second_gain, second_unit, second_inv)
    grad_down_bias = jnp.sum(grad_second, axis=0)
    grad_second_low = links.to_own_order(chip_tokens(grad_second.astype(bf16)), 1)
    grad_active = dot(grad_second_low, w_down)
    grad_up = jax.vjp(gelu_exact, up_proj)[1](grad_active)[0]
    grad_up_bias = jnp.sum(grad_up, axis=0)
    grad_up_low = grad_up.astype(bf16)
    sum_down = links.scatter(cross_dot(grad_second_low, active).astype(bf16))
    grad_normed = grad_second + links.to_plain_order(sum_cores(trans_dot(grad_up_low, w_up)), 1)
    sum_up = links.scatter(cross_dot(normed_low, grad_up_low).astype(bf16))
    grad_first_gain = jnp.sum(grad_normed * first_unit, axis=0)
    grad_first_shift = jnp.sum(grad_normed, axis=0)
    grad_first = norm_back(grad_normed * first_gain, first_unit, first_inv)
    grad_output_bias = jnp.sum(grad_first, axis=0)
    grad_first_half = halves(chip_tokens(grad_first.astype(bf16)))[0]
    sum_out = links.scatter(cross_dot(context, grad_first_half).astype(bf16))
    grad_context = links.to_plain_order(trans_dot(grad_first_half, w_out), 1)
    mine, theirs = halves(grad_context)
    theirs = links.swap_core(theirs)
    theirs = jnp.concatenate([theirs[row_count:], theirs[:row_count]], axis=0)
    grad_context = (mine + theirs).astype(bf16).reshape(head_shape)
    grad_query, grad_keys, grad_values = attend_back(
        query_rows, key_rows, values, seg, log_total, grad_context
    )
    flat_shape = (2 * row_count, hw)
    grad_query = grad_query.reshape(flat_shape)
    grad_values = grad_values.reshape(flat_shape)
    grad_mixed = jnp.concatenate(
        [grad_query, grad_keys.reshape(flat_shape), grad_values], axis=1
    ).astype(bf16)
    sum_qkv = links.scatter(cross_dot(rows_in, grad_mixed).astype(bf16))
    grad_input = grad_first + links.to_plain_order(sum_cores(trans_dot(grad_mixed, w_qkv)), 1)

    zeros_half = jnp.zeros((hw,), f32)
    zeros_hidden = jnp.zeros((hh,), f32)
    grad_small = jnp.concatenate(
        [
            both(jnp.sum(grad_query, axis=0), zeros_half, 0)[None],
            both(jnp.sum(grad_values, axis=0), zeros_half, 0)[None],
            grad_output_bias[None],
            grad_first_gain[None],
            grad_first_shift[None],
            both(grad_up_bias, zeros_hidden, 0).reshape(-1, width),
            grad_down_bias[None],
            grad_second_gain[None],
            grad_second_shift[None],
        ],
        axis=0,
    )
    grad_small = links.sum_all(grad_small)
    grad_small = lax.dynamic_slice_in_dim(
        grad_small, lax.axis_index("shard") * own_rows, own_rows, 1
    ).T

    def owned_sum(value, pieces):
        mine = pick(value[:own_rows], value[own_rows:])
        theirs = links.swap_core(pick(value[own_rows:], value[:own_rows]))
        mine = mine.reshape(own_rows, pieces, -1)
        theirs = theirs.reshape(own_rows, pieces, -1)
        value = both(mine, theirs, 2).reshape(own_rows, -1)
        total = value.astype(f32)
        bit = 1
        while bit < rep_count:
            low = total.astype(bf16)
            total = low.astype(f32) + links.swap_rep(low, bit).astype(f32)
            bit *= 2
        return total

    grad_wide = jnp.concatenate(
        [
            owned_sum(sum_qkv, 3),
            owned_sum(sum_out, 1),
            owned_sum(sum_up, 1),
            owned_sum(sum_down, 1),
        ],
        axis=1,
    )
    new_w, new_wm, new_wv = adam_step(
        weights, weight_m, weight_v, grad_wide, matrix_rate, weight_decay
    )
    new_vec, new_vm, new_vv = adam_step(vectors, vector_m, vector_v, grad_small, vector_rate, 0.0)
    return (
        output,
        grad_input,
        grad_wide,
        new_w,
        new_wm,
        new_wv,
        grad_small,
        new_vec,
        new_vm,
        new_vv,
    )


def solution(mesh):
    rep_count, shard_count = mesh.shape["rep"], mesh.shape["shard"]
    tokens = P(("rep", "shard"), None)
    owned = P("shard", None)

    def local(*args):
        return body(*args, rep_count=rep_count, shard_count=shard_count)

    return jax.shard_map(
        local,
        mesh=mesh,
        in_specs=(tokens, tokens, P(("rep", "shard"))) + (owned,) * 6,
        out_specs=(tokens, tokens) + (owned,) * 8,
        check_vma=False,
    )
```
